32 devices in a mesh: table: 4 (over y, core), batch: 8 (over z, x).
Axes of the slice: x: 2, y: 2, z: 4, core: 2. Of those that a mesh axis runs over, the one named last changes fastest.
Arguments:
- emb: bfloat16 [4, 262144, 128], P('table', 'batch'), may hold values from -6 to 6
- short_rows: int32 [192, 4, 32], P(('table', 'batch')), may hold values from 0 to 262143
- short_len: int32 [192, 4], P(('table', 'batch')), may hold values from 1 to 32
- short_sample: int32 [192, 4], P(('table', 'batch')), may hold values from 0 to 7, as said below
- long_rows: int32 [64, 4, 512], P(('table', 'batch')), may hold values from 0 to 262143, as said below
- long_len: int32 [64, 4], P(('table', 'batch')), may hold values from 33 to 500, as said below
- long_sample: int32 [64, 4], P(('table', 'batch')), may hold values from 0 to 7, as said below
Outputs:
- pooled: float32 [256, 4, 128], P(('table', 'batch'))
The draws below stay inside these ranges and needn't reach their ends.
Inputs may be any that keep to these rules, and one draw needn't show every extreme that they name: For each block of 6 short bags and 2 long bags with the same j // 6 and j // 2, and each table, short_sample and long_sample together name each of the 8 samples exactly once. `long_sample`: see short_sample. `long_rows`: within one bag no row id stands more than 256 times among the first long_len positions, and in every draw some bag has a row id that stands exactly that often. `long_len`: in every draw some long bag has length 500.
All inputs are finite; a program needn't handle non-finite values.
Results may differ from the reference program's by a relative error of at most 0.0003.
Values sent between devices are 32-bit elements; how exact they have to be, the bound alone decides.
A program may use at most 64 MiB of HBM per device.

```python
import jax
import jax.numpy as jnp
from jax import lax

E = 128
B_DEV = 8
WS = 32
WL = 512
MAXLEN = 500
LONG_DEV = 2
SHORT_DEV = 6
R = 262144
NT = 4
B = 256
DEVICES = 32


def bag_order(key):
    scores = jax.random.randint(jax.random.fold_in(key, 7), (DEVICES, NT, B_DEV), 0, 1 << 20, dtype=jnp.int32)
    scores = scores * B_DEV + jnp.arange(B_DEV, dtype=jnp.int32)
    return jnp.argsort(scores, axis=2).astype(jnp.int32)


def draw_short_sample(key, part):
    order = bag_order(key)[:, :, :SHORT_DEV]
    return jnp.transpose(order, (0, 2, 1)).reshape(DEVICES * SHORT_DEV, NT)


def draw_long_sample(key, part):
    order = bag_order(key)[:, :, SHORT_DEV:]
    return jnp.transpose(order, (0, 2, 1)).reshape(DEVICES * LONG_DEV, NT)


def long_bags(key):
    bag_count = DEVICES * LONG_DEV
    total = bag_count * NT
    ceiling = min(256, MAXLEN)
    middle_low = min(17, ceiling)
    middle_high = min(255, ceiling)
    base = jax.random.fold_in(key, 11)
    lengths = jax.random.randint(jax.random.fold_in(base, 1), (bag_count, NT), WS + 1, MAXLEN + 1, dtype=jnp.int32)
    bag_rank = jax.random.permutation(jax.random.fold_in(base, 2), total).astype(jnp.int32).reshape(bag_count, NT)
    middle = jax.random.randint(jax.random.fold_in(base, 3), (bag_count, NT), middle_low, middle_high + 1, dtype=jnp.int32)
    repeats = jnp.where(bag_rank == 0, ceiling, jnp.where(bag_rank <= 15, middle, 0)).astype(jnp.int32)
    lengths = jnp.where(bag_rank == 0, MAXLEN, jnp.maximum(lengths, repeats)).astype(jnp.int32)
    chosen = jax.random.randint(jax.random.fold_in(base, 4), (bag_count, NT), 0, R, dtype=jnp.int32)
    others = jax.random.randint(jax.random.fold_in(base, 5), (bag_count, NT, WL), 0, R - 1, dtype=jnp.int32)
    others = (chosen[:, :, None] + 1 + others) % R
    place = jnp.arange(WL, dtype=jnp.int32)[None, None, :]
    scores = jax.random.randint(jax.random.fold_in(base, 6), (bag_count, NT, WL), 0, 1 << 20, dtype=jnp.int32)
    scores = scores * WL + place
    scores = jnp.where(place < lengths[:, :, None], scores, scores + (1 << 30))
    order = jnp.argsort(scores, axis=2).astype(jnp.int32)
    position_rank = jnp.argsort(order, axis=2).astype(jnp.int32)
    rows = jnp.where(position_rank < repeats[:, :, None], chosen[:, :, None], others)
    return (rows.astype(jnp.int32), lengths.astype(jnp.int32))


def draw_long_rows(key, part):
    return long_bags(key)[0]


def draw_long_len(key, part):
    return long_bags(key)[1]


def plant(entries, rng, least, largest):
    dims = entries.shape
    spot = [jax.random.randint(jax.random.fold_in(rng, axis), (), 0, dims[axis]) for axis in range(len(dims))]
    entries = entries.at[tuple(spot)].set(least)
    longest = dims.index(max(dims))
    spot[longest] = (spot[longest] + 1) % dims[longest]
    return entries.at[tuple(spot)].set(largest)


def levels(own_key, dims, split, low, high):
    level, own = 1.0, jax.random.fold_in(own_key, 6)
    for dim, parts in split:
        steps = jnp.exp(jax.random.uniform(jax.random.fold_in(own, dim), (parts,), jnp.float32, low / len(split), high / len(split)))
        level = level * jnp.repeat(steps, dims[dim] // parts).reshape([-1 if axis == dim else 1 for axis in range(len(dims))])
    return level


def noise(own_key, shape, scale, reach, cuts=(), kind=jnp.bfloat16):
    result = jax.random.normal(own_key, shape, jnp.float32) * scale
    if len(cuts) > 0:
        result = levels(own_key, shape, cuts, -0.22, 0.18) * result
    return jnp.clip(result, min=-reach, max=reach).astype(kind)


def setup_inputs(seed: int = 0) -> dict:
    seeds = jax.random.split(jax.random.key(seed), 8)
    emb = noise(seeds[0], (NT, R, E), 1.0, 6.0, ((0, 4), (1, 8)))
    short_rows = plant(jax.random.randint(seeds[1], (DEVICES * SHORT_DEV, NT, WS), 0, R), jax.random.fold_in(seeds[1], 1), 0, R - 1).astype(jnp.int32)
    short_len = plant(jax.random.randint(seeds[2], (DEVICES * SHORT_DEV, NT), 1, WS + 1), jax.random.fold_in(seeds[2], 1), 1, WS).astype(jnp.int32)
    short_sample = draw_short_sample(jax.random.fold_in(seeds[7], 71), 0)
    long_rows = draw_long_rows(jax.random.fold_in(seeds[7], 71), 0)
    long_len = draw_long_len(jax.random.fold_in(seeds[7], 71), 0)
    long_sample = draw_long_sample(jax.random.fold_in(seeds[7], 71), 0)
    return {"emb": emb, "short_rows": short_rows, "short_len": short_len, "short_sample": short_sample, "long_rows": long_rows, "long_len": long_len, "long_sample": long_sample}


def bag_sums(table, rows, lengths):
    place = jnp.arange(rows.shape[1], dtype=jnp.int32)
    valid = place[None, :] < lengths[:, None]
    picked = table[rows].astype(jnp.float32)
    total = lax.optimization_barrier(jnp.sum(jnp.where(valid[:, :, None], picked, jnp.float32(0.0)), axis=1))
    return total / jnp.sqrt(lengths.astype(jnp.float32))[:, None]

def reference(emb, short_rows, short_len, short_sample, long_rows, long_len, long_sample):
    pooled = jnp.zeros((B, NT, E), jnp.float32)
    short_owner = jnp.arange(DEVICES * SHORT_DEV, dtype=jnp.int32) // SHORT_DEV * B_DEV
    long_owner = jnp.arange(DEVICES * LONG_DEV, dtype=jnp.int32) // LONG_DEV * B_DEV
    for table_id in range(NT):
        short_vec = bag_sums(emb[table_id], short_rows[:, table_id, :], short_len[:, table_id])
        pooled = pooled.at[short_owner + short_sample[:, table_id], table_id].set(short_vec)
        long_vec = bag_sums(emb[table_id], long_rows[:, table_id, :], long_len[:, table_id])
        pooled = pooled.at[long_owner + long_sample[:, table_id], table_id].set(long_vec)
    return pooled
```

```python
import jax
import jax.numpy as jnp
from jax import lax
from jax.sharding import PartitionSpec as P

AXES = ("table", "batch")


def mask_rows(rows, lengths):
    place = lax.broadcasted_iota(jnp.int32, rows.shape, 2)
    return jnp.where(place < lengths[:, :, None], rows, -1)


def split_keys(keys, row_base, rows_dev):
    local = keys - row_base
    inside = (local >= 0) & (local < rows_dev)
    high = jnp.where(inside, local // 128, -1)
    low = jnp.where(inside, local % 128, -1)
    low_hot = (low[:, :, None] == lax.broadcasted_iota(jnp.int32, (1, 1, 128), 2)).astype(
        jnp.bfloat16
    )
    return high, low_hot


def count_block(high, low_hot, index, high_count):
    targets = index * high_count + lax.broadcasted_iota(jnp.int32, (1, 1, high_count), 2)
    high_hot = (high[:, :, None] == targets).astype(jnp.bfloat16)
    counts = jnp.einsum("bwh,bwl->bhl", high_hot, low_hot, preferred_element_type=jnp.float32)
    return counts.astype(jnp.bfloat16).reshape(high.shape[0], high_count * 128)


def pool_rows(short_keys, long_keys, table, row_base):
    rows_dev = table.shape[0]
    block = min(8192, rows_dev)
    high_count = block // 128
    short_split = split_keys(short_keys, row_base, rows_dev)
    long_split = split_keys(long_keys, row_base, rows_dev)
    bag_count = short_keys.shape[0] + long_keys.shape[0]

    def add_block(index, total):
        counts = jnp.concatenate(
            [
                count_block(*short_split, index, high_count),
                count_block(*long_split, index, high_count),
            ],
            axis=0,
        )
        piece = lax.dynamic_slice_in_dim(table, index * block, block, 0)
        return total + jnp.dot(counts, piece, preferred_element_type=jnp.float32)

    start = jnp.zeros((bag_count, table.shape[1]), jnp.float32)
    return lax.fori_loop(0, rows_dev // block, add_block, start)


def place_bags(values, lengths, samples, sample_count):
    scaled = values / jnp.sqrt(lengths.astype(jnp.float32))[:, :, None]
    slots = lax.broadcasted_iota(jnp.int32, samples.shape + (sample_count,), 2)
    picks = (samples[:, :, None] == slots).astype(jnp.float32)
    return jnp.sum(picks[:, :, :, None] * scaled[:, :, None, :], axis=0)


def on_device(emb, short_rows, short_len, short_sample, long_rows, long_len, long_sample):
    tables = lax.axis_size("table")
    batch = lax.axis_size("batch")
    devices = tables * batch
    short_dev, _, short_width = short_rows.shape
    long_dev, _, long_width = long_rows.shape
    width = emb.shape[2]
    short_flat = jnp.transpose(mask_rows(short_rows, short_len), (1, 0, 2)).reshape(tables, -1)
    long_flat = jnp.transpose(mask_rows(long_rows, long_len), (1, 0, 2)).reshape(tables, -1)
    keys = jnp.concatenate([short_flat, long_flat], axis=1)
    keys = jnp.broadcast_to(keys[:, None, :], (tables, batch, keys.shape[1]))
    keys = keys.reshape(devices, -1)
    keys = lax.all_to_all(keys, AXES, split_axis=0, concat_axis=0, tiled=True)
    short_all = keys[:, : short_dev * short_width].reshape(devices * short_dev, short_width)
    long_all = keys[:, short_dev * short_width :].reshape(devices * long_dev, long_width)
    row_base = lax.axis_index("batch") * emb.shape[1]
    part = pool_rows(short_all, long_all, emb[0], row_base)
    short_part = part[: devices * short_dev].reshape(devices, short_dev, width)
    long_part = part[devices * short_dev :].reshape(devices, long_dev, width)
    part = jnp.concatenate([short_part, long_part], axis=1)
    part = lax.all_to_all(part, AXES, split_axis=0, concat_axis=0, tiled=True)
    sums = jnp.sum(part.reshape(tables, batch, short_dev + long_dev, width), axis=1)
    sums = jnp.transpose(sums, (1, 0, 2))
    lengths = jnp.concatenate([short_len, long_len], axis=0)
    samples = jnp.concatenate([short_sample, long_sample], axis=0)
    pooled = place_bags(sums, lengths, samples, samples.shape[0])
    return jnp.transpose(pooled, (1, 0, 2))


def solution(mesh):
    return jax.shard_map(
        on_device,
        mesh=mesh,
        in_specs=(
            P("table", "batch", None),
            P(("table", "batch"), None, None),
            P(("table", "batch"), None),
            P(("table", "batch"), None),
            P(("table", "batch"), None, None),
            P(("table", "batch"), None),
            P(("table", "batch"), None),
        ),
        out_specs=P(("table", "batch"), None, None),
        check_vma=False,
    )
```
